512 devices in a mesh: leaf: 32 (over z, x), brick: 16 (over y, core).
Axes of the slice: x: 4, y: 8, z: 8, core: 2. Of those that a mesh axis runs over, the one named last changes fastest.
Arguments:
- points: bfloat16 [64, 32, 2, 3, 256], P('leaf', 'brick'), may hold values from 0 to 1
- test_matrix: bfloat16 [64, 32, 2, 64, 256], P('leaf', 'brick'), may hold values from -40 to 40
- trunc_ranks: int32 [5], replicated, may hold values from 32 to 64, as said below
Outputs:
- leaf_basis: bfloat16 [64, 32, 2, 64, 256], P('leaf', 'brick')
- leaf_transfer: float32 [64, 32, 2, 64, 64], P('leaf', 'brick')
- upper_transfer: float32 [3, 32, 16, 64, 64], P(None, 'leaf', 'brick')
- top_sample: float32 [32, 16, 64, 64], P('leaf', 'brick')
The draws below stay inside these ranges and needn't reach their ends.
Inputs may be any that keep to these rules, and one draw needn't show every extreme that they name: `trunc_ranks`: one level keeps 64 rows and another keeps 64 // 2.
All inputs are finite; a program needn't handle non-finite values.
Results may differ from the reference program's by a relative error of at most 0.0085.
The reference program's roundings to bfloat16 on the way (of `kernel_tile`) count: a program that leaves them out, or rounds other values in their place, can miss the bound.
Values may be sent and summed in bfloat16 or wider, within the bound.
No kernel may reach another device: no remote copies, remote signals or barrier semaphores. Data moves between devices by JAX's collectives and lax.ppermute only.
A program may use at most 64 MiB of HBM per device.

```python
import math
import jax
import jax.numpy as jnp
from jax import lax

LEAF = 256
SAMPLES = 64
LEVELS = 4
NZ = 2
NX = 64
NY = 32
N_LEAF = 32
N_BRICK = 16


def draw_test_matrix(key, part):
    key_base = jax.random.fold_in(key, 11)
    key_scale = jax.random.fold_in(key, 12)
    shape_all = (NX, NY, NZ, SAMPLES, LEAF)
    raw_values = jnp.clip(jax.random.normal(key_base, shape_all, jnp.float32), -4.0, 4.0)
    spread = jnp.exp(jax.random.uniform(key_scale, (NX, NY, NZ, SAMPLES, 1), jnp.float32, 0.0, math.log(10.0)))
    return (raw_values * spread).astype(jnp.bfloat16)


def draw_trunc_ranks(key, part):
    key_order = jax.random.fold_in(key, 21)
    key_value = jax.random.fold_in(key, 22)
    order_list = jax.random.permutation(key_order, LEVELS + 1)
    values_all = jax.random.randint(key_value, (LEVELS + 1,), SAMPLES // 2, SAMPLES + 1, dtype=jnp.int32)
    values_all = values_all.at[order_list[0]].set(SAMPLES)
    values_all = values_all.at[order_list[1]].set(SAMPLES // 2)
    return values_all


def block_levels(key, dims, pieces, least, largest):
    gain = 1.0
    for position, blocks in pieces:
        draws = jax.random.uniform(jax.random.fold_in(jax.random.fold_in(key, 6), position), (blocks,), jnp.float32, least / len(pieces), largest / len(pieces))
        gain = gain * jnp.repeat(jnp.exp(draws), dims[position] // blocks).reshape((-1,) + (1,) * (len(dims) - 1 - position))
    return gain


def setup_inputs(seed: int = 0) -> dict:
    key_list = jax.random.split(jax.random.key(seed), 4)
    points = jnp.clip(1.0 * jax.random.uniform(key_list[0], (NX, NY, NZ, 3, LEAF), jnp.float32) ** block_levels(key_list[0], (NX, NY, NZ, 3, LEAF), ((0, 32), (1, 16)), -0.2, 0.2), 0.0, 1.0).astype(jnp.bfloat16)
    test_matrix = draw_test_matrix(jax.random.fold_in(key_list[3], 71), 0)
    trunc_ranks = draw_trunc_ranks(jax.random.fold_in(key_list[3], 71), 0)
    return dict(points=points, test_matrix=test_matrix, trunc_ranks=trunc_ranks)


ROOT_THREE = math.sqrt(3.0)
SHIFT_SHARE = 0.01
TINY = 1e-06
HIGH = lax.Precision.HIGHEST
NEIGHBOUR_OFFSETS = [(off_x, off_y, off_z) for off_x in (-1, 0, 1) for off_y in (-1, 0, 1) for off_z in (-1, 0, 1)]

def matern(near_points, own_points, offset):
    summed = 0.0
    for axis_id in range(3):
        spacing = offset[axis_id] + near_points[..., axis_id, :, None] - own_points[..., axis_id, None, :]
        summed = summed + spacing * spacing
    scaled = ROOT_THREE * jnp.sqrt(summed)
    return (1.0 + scaled) * jnp.exp(-scaled)

def factor(gram_sum):
    trace_sum = jnp.trace(gram_sum, axis1=-2, axis2=-1)
    shift_term = SHIFT_SHARE * trace_sum / gram_sum.shape[-1] + TINY
    identity = jnp.eye(gram_sum.shape[-1], dtype=gram_sum.dtype)
    factor_low = jnp.linalg.cholesky(gram_sum + shift_term[..., None, None] * identity)
    return (factor_low, trace_sum)

def solve_low(factor_low, right_side):
    return jax.scipy.linalg.solve_triangular(factor_low, right_side, lower=True)

def keep_rows(trunc_ranks, height, sample_width):
    return (jnp.arange(sample_width, dtype=jnp.int32) < trunc_ranks[height]).astype(jnp.float32)[:, None]

def leaf_level(sample, keep):
    gram_sum = jnp.einsum('...sp,...tp->...st', sample, sample, precision=HIGH)
    factor_low, trace_sum = factor(gram_sum)
    basis_rows = solve_low(factor_low, sample) * keep
    projected = solve_low(factor_low, gram_sum) * keep
    return (basis_rows, projected)

def merge_level(projected, keep):
    grid_x, grid_y, grid_z = (projected.shape[0], projected.shape[1], projected.shape[2])
    sample_width = projected.shape[-1]
    fold_x = 2 if grid_x > 1 else 1
    fold_y = 2 if grid_y > 1 else 1
    fold_z = 2 if grid_z > 1 else 1
    children = projected.reshape(grid_x // fold_x, fold_x, grid_y // fold_y, fold_y, grid_z // fold_z, fold_z, sample_width, sample_width)
    gram_sum = jnp.einsum('aibjcksu,aibjcksv->abcuv', children, children, precision=HIGH)
    factor_low, trace_sum = factor(gram_sum)
    spread = jnp.broadcast_to(factor_low[:, None, :, None, :, None], children.shape)
    transfer = solve_low(spread, jnp.swapaxes(children, -1, -2)) * keep
    transfer = transfer.reshape(projected.shape)
    parent = solve_low(factor_low, gram_sum) * keep
    return (transfer, parent, trace_sum)

def near_samples(points, test_matrix):
    own_all = points.astype(jnp.float32)
    widths = ((1, 1), (1, 1), (1, 1), (0, 0), (0, 0))
    padded_points = jnp.pad(own_all, widths)
    padded_tests = jnp.pad(test_matrix, widths)
    grid_y, grid_z = (points.shape[1], points.shape[2])

    def one_row(row_index):
        own_points = lax.dynamic_index_in_dim(own_all, row_index, 0, keepdims=False)
        running = jnp.zeros((grid_y, grid_z, test_matrix.shape[3], points.shape[4]), jnp.float32)
        for off_x, off_y, off_z in NEIGHBOUR_OFFSETS:
            point_slab = lax.dynamic_index_in_dim(padded_points, row_index + 1 + off_x, 0, keepdims=False)
            test_slab = lax.dynamic_index_in_dim(padded_tests, row_index + 1 + off_x, 0, keepdims=False)
            near_points = point_slab[1 + off_y:1 + off_y + grid_y, 1 + off_z:1 + off_z + grid_z]
            near_tests = test_slab[1 + off_y:1 + off_y + grid_y, 1 + off_z:1 + off_z + grid_z]
            kernel_tile = matern(near_points, own_points, (float(off_x), float(off_y), float(off_z))).astype(jnp.bfloat16)
            kernel_tile = lax.optimization_barrier(kernel_tile)
            running = running + jnp.einsum('yzsq,yzqp->yzsp', near_tests.astype(jnp.float32), kernel_tile.astype(jnp.float32), precision=HIGH)
        return running
    return lax.map(one_row, jnp.arange(points.shape[0], dtype=jnp.int32))

def reference(points, test_matrix, trunc_ranks):
    sample = near_samples(points, test_matrix)
    sample_width = sample.shape[-2]
    scale_up = math.sqrt(sample_width)
    basis_rows, projected = leaf_level(sample, keep_rows(trunc_ranks, 0, sample_width))
    leaf_basis = (basis_rows * math.sqrt(points.shape[-1])).astype(jnp.bfloat16)
    leaf_transfer = None
    uppers = []
    trace_sum = None
    for height in range(1, LEVELS + 1):
        transfer, projected, trace_sum = merge_level(projected, keep_rows(trunc_ranks, height, sample_width))
        if height == 1:
            leaf_transfer = transfer * scale_up
        else:
            stride = 2 ** (height - 2)
            rows_pick = jnp.arange(N_LEAF, dtype=jnp.int32) // stride
            cols_pick = jnp.arange(N_BRICK, dtype=jnp.int32) // stride
            uppers.append(transfer[rows_pick][:, cols_pick][:, :, 0] * scale_up)
    stride = 2 ** (LEVELS - 1)
    rows_pick = jnp.arange(N_LEAF, dtype=jnp.int32) // stride
    cols_pick = jnp.arange(N_BRICK, dtype=jnp.int32) // stride
    top_parent = projected[rows_pick][:, cols_pick][:, :, 0]
    top_trace = trace_sum[rows_pick][:, cols_pick][:, :, 0]
    top_sample = top_parent / jnp.sqrt(top_trace / sample_width + TINY)[..., None, None]
    return (leaf_basis, leaf_transfer, jnp.stack(uppers), top_sample)
```

```python
import functools
import math

import jax
import jax.numpy as jnp
from jax import lax
from jax.experimental import pallas as pl
from jax.experimental.pallas import tpu as pltpu
from jax.sharding import PartitionSpec as P

LEVELS = 4
EXP_SCALE = -1.0 / math.log(2.0)
AHEAD = 1
BEHIND = 1
SHIFT_SHARE = 0.01
TINY = 1e-06
HIGH = lax.Precision.HIGHEST
F32 = jnp.float32
BF16 = jnp.bfloat16
S = 64
N = 256
FEAT = 32
LEAF_PAIRS = 4
LEAF_PANEL = 4
ONE_PANEL = 8


def split_square(x):
    sq = x * x
    hi = sq.astype(BF16).astype(F32)
    return hi, sq - hi


def left_rows(pts):
    x = pts.astype(F32)
    hi, lo = split_square(x)
    threes = jnp.full((10, N), 3.0, F32)
    zeros = jnp.zeros((FEAT - 25, N), F32)
    return jnp.concatenate([-2.0 * x, -2.0 * x, hi, lo, x, threes, zeros], axis=0)


def right_rows(pts):
    x = pts.astype(F32)
    hi, lo = split_square(x)
    tripled = 3.0 * x
    coarse = tripled.astype(BF16).astype(F32)
    zero3 = jnp.zeros((3, N), F32)
    three3 = jnp.full((3, N), 3.0, F32)
    tail = jnp.zeros((FEAT - 25, N), F32)
    base = jnp.concatenate(
        [coarse, tripled - coarse, three3, three3, zero3, hi, lo, zero3, zero3[:1], tail], axis=0
    )
    slope = jnp.concatenate(
        [zero3] * 4 + [2.0 * three3, zero3, zero3, -2.0 * x, zero3[:1] + 1.0, tail], axis=0
    )
    return base, slope


def put_left(pts, left_ref, slot):
    left_ref[slot] = left_rows(pts).T.astype(BF16)


def put_right(pts, base_ref, slope_ref, slot):
    base, slope = right_rows(pts)
    base_ref[slot] = base
    slope_ref[slot] = slope


def offset_rows(off):
    row = lax.broadcasted_iota(jnp.int32, (FEAT, N), 0)
    ox, oy, oz = (jnp.asarray(o, F32) for o in off)
    total = ox * ox + oy * oy + oz * oz
    out = jnp.where((row == 12) | (row == 21), ox, total)
    out = jnp.where((row == 13) | (row == 22), oy, out)
    return jnp.where((row == 14) | (row == 23), oz, out)


def square_tile(left, base, slope, off):
    right = (base + offset_rows(off) * slope).astype(BF16)
    return jnp.dot(left, right, preferred_element_type=F32)


def matern(sq):
    sq = jnp.maximum(sq, 1e-30)
    scaled = sq * lax.rsqrt(sq)
    return ((1.0 + scaled) * jnp.exp2(scaled * EXP_SCALE)).astype(BF16)


def pipelined(squares, uses):
    ahead = [squares[k]() for k in range(min(AHEAD, len(squares)))]
    waiting = []
    for k in range(len(squares)):
        if k + AHEAD < len(squares):
            ahead.append(squares[k + AHEAD]())
        waiting.append((uses[k], matern(ahead.pop(0))))
        if len(waiting) > BEHIND:
            use, tile = waiting.pop(0)
            use(tile)
    for use, tile in waiting:
        use(tile)


def bits(box):
    return box >> 2, (box >> 1) & 1, box & 1


def own_pairs_body(pts_ref, tst_ref, out_ref, left_ref, base_ref, slope_ref):
    for b in range(8):
        put_left(pts_ref[b], left_ref, b)
        put_right(pts_ref[b], base_ref, slope_ref, b)
        out_ref[b] = jnp.zeros((S, N), F32)

    def square(n, b):
        nx, ny, nz = bits(n)
        bx, by, bz = bits(b)
        return square_tile(left_ref[n], base_ref[b], slope_ref[b], (nx - bx, ny - by, nz - bz))

    def use(n, b, both, tile):
        out_ref[b] = out_ref[b] + jnp.dot(tst_ref[n], tile, preferred_element_type=F32)
        if both:
            out_ref[n] = out_ref[n] + lax.dot_general(
                tst_ref[b], tile, (((1,), (1,)), ((), ())), preferred_element_type=F32
            )

    def step(i, carry):
        pairs = [
            ((first + shift) & 7, first, shift > 0) for first in (i, i + 4) for shift in range(4)
        ]
        pairs.append((i + 4, i, True))
        pipelined(
            [functools.partial(square, n, b) for n, b, _ in pairs],
            [functools.partial(use, n, b, both) for n, b, both in pairs],
        )
        return carry

    lax.fori_loop(0, 4, step, 0)


def vmem(shape, dtype):
    return pltpu.VMEM(shape, dtype)


def near(value):
    return pltpu.with_memory_space_constraint(value, pltpu.VMEM)


def own_pairs(points, tests):
    return pl.pallas_call(
        own_pairs_body,
        out_shape=vmem((8, S, N), F32),
        scratch_shapes=[
            vmem((8, N, FEAT), BF16),
            vmem((8, FEAT, N), F32),
            vmem((8, FEAT, N), F32),
        ],
        name="own_pairs",
    )(points, tests)


def halo_tiles(jobs, own, part_ref, out_ref, left_ref, halo_ref, base_ref, slope_ref):
    totals = [part_ref[own + bz] for bz in range(2)]

    def square(slot, box, bz, off):
        return square_tile(left_ref[slot], base_ref[own + bz], slope_ref[own + bz], off)

    def use(slot, box, bz, off, tile):
        tests = halo_ref[box, :S, :]
        totals[bz] = totals[bz] + jnp.dot(tests, tile, preferred_element_type=F32)

    pipelined(
        [functools.partial(square, *job) for job in jobs],
        [functools.partial(use, *job) for job in jobs],
    )
    for bz in range(2):
        out_ref[own + bz] = totals[bz]


def halo_prep(pts_ref, sides, left_ref, base_ref, slope_ref):
    count = sides[0].shape[0]
    for side, ref in enumerate(sides):
        for box in range(count):
            put_left(ref[box, S : S + 3, :], left_ref, side * count + box)
    for b in range(8):
        put_right(pts_ref[b], base_ref, slope_ref, b)


def halo_x_body(pts_ref, low_ref, high_ref, part_ref, out_ref, left_ref, base_ref, slope_ref):
    sides = (low_ref, high_ref)
    halo_prep(pts_ref, sides, left_ref, base_ref, slope_ref)
    for i, side in enumerate(sides):

        def step(j, carry):
            jobs = [
                (i * 4 + ny * 2 + nz, ny * 2 + nz, bz, (2 * i - 1, ny - j, nz - bz))
                for bz in range(2) for ny in range(2) for nz in range(2)
            ]
            halo_tiles(
                jobs, i * 4 + j * 2, part_ref, out_ref, left_ref, side, base_ref, slope_ref
            )
            return carry

        lax.fori_loop(0, 2, step, 0)


def halo_x(points, low, high, part):
    return pl.pallas_call(
        halo_x_body,
        out_shape=vmem((8, S, N), F32),
        in_specs=[vmem_spec()] * 4,
        scratch_shapes=[
            vmem((8, N, FEAT), BF16),
            vmem((8, FEAT, N), F32),
            vmem((8, FEAT, N), F32),
        ],
        name="halo_x",
    )(points, near(low), near(high), near(part))


def spread_row(block, row):
    return jnp.broadcast_to(block[row : row + 1, :], block.shape)


def minus(blocks, mults, row):
    return [b - m * row for b, m in zip(blocks, mults)]


def eliminate(groups, lane_of, panel):
    groups = [[list(blocks) for blocks in group] for group in groups]
    sub = lax.broadcasted_iota(jnp.int32, (8, 128), 0)
    for kb in range(8):
        diags = [jnp.ones((8, 128), F32) for _ in groups]
        for start in range(0, 8, panel):
            lanes = [lane_of(kb * 8 + start + j) for j in range(panel)]
            panels = [
                [
                    [jnp.take_along_axis(group[0][r], lane, axis=1) for r in range(kb, 8)]
                    for lane in lanes
                ]
                for group in groups
            ]
            for j in range(0, panel, 2):
                s = start + j
                for p, (group, cols) in enumerate(zip(groups, panels)):
                    one, two = cols[j], cols[j + 1]
                    a00 = spread_row(one[0], s)
                    a01 = spread_row(two[0], s)
                    a11 = spread_row(two[0], s + 1)
                    root0 = lax.rsqrt(a00)
                    root1 = lax.rsqrt(a00 * a11 - a01 * a01)
                    inv0 = root0 * root0
                    inv1 = (root1 * root1) * a00
                    m0 = [c * inv0 for c in one]
                    m0[0] = jnp.where(sub > s, m0[0], 0.0)
                    two = minus(two, m0, a01)
                    m1 = [c * inv1 for c in two]
                    m1[0] = jnp.where(sub > s + 1, m1[0], 0.0)
                    diags[p] = jnp.where(
                        sub == s, one[0], jnp.where(sub == s + 1, two[0], diags[p])
                    )
                    for jj in range(j + 2, panel):
                        cols[jj] = minus(cols[jj], m0, spread_row(cols[jj][0], s))
                        cols[jj] = minus(cols[jj], m1, spread_row(cols[jj][0], s + 1))
                    for blocks in group:
                        blocks[kb:] = minus(blocks[kb:], m0, spread_row(blocks[kb], s))
                        blocks[kb:] = minus(blocks[kb:], m1, spread_row(blocks[kb], s + 1))
        for p, group in enumerate(groups):
            root = lax.rsqrt(diags[p])
            for blocks in group:
                blocks[kb] = blocks[kb] * root
    return groups


def row_blocks(value):
    return [value[r * 8 : r * 8 + 8, :] for r in range(8)]


def total(value):
    return jnp.sum(jnp.sum(value, axis=0, keepdims=True), axis=1, keepdims=True)


def factor_one(gram, rank):
    row = lax.broadcasted_iota(jnp.int32, (S, S), 0)
    col = lax.broadcasted_iota(jnp.int32, (S, S), 1)
    eye = row == col
    trace = total(jnp.where(eye, gram, 0.0))
    shift = SHIFT_SHARE * trace / S + TINY
    shifted = gram + jnp.where(eye, shift, 0.0)
    both = jnp.concatenate([shifted, jnp.where(eye, 1.0, 0.0).astype(F32)], axis=1)
    done = eliminate(
        [[row_blocks(both)]], lambda k: jnp.full((8, 128), k, jnp.int32), ONE_PANEL
    )
    both = jnp.concatenate(done[0][0], axis=0)
    inverse = both[:, S:]
    upper = jnp.where(col >= row, both[:, :S], 0.0)
    projected = jnp.where(row < rank, upper - shift * inverse, 0.0)
    return inverse, projected, trace


def factor_pairs(grams, rank):
    row = lax.broadcasted_iota(jnp.int32, (S, 128), 0)
    lane = lax.broadcasted_iota(jnp.int32, (S, 128), 1)
    first = lane < S
    col = lane & (S - 1)
    eye = row == col
    ident = jnp.where(eye, 1.0, 0.0).astype(F32)
    half = lax.broadcasted_iota(jnp.int32, (8, 128), 1) & S
    shifts, groups = [], []
    for gram in grams:
        packed = jnp.where(first, gram[:S], gram[S:])
        diag = jnp.where(eye, packed, 0.0)
        traces = total(jnp.where(first, diag, 0.0)), total(jnp.where(first, 0.0, diag))
        shift = [SHIFT_SHARE * t / S + TINY for t in traces]
        shift = jnp.where(first, shift[0], shift[1])
        shifts.append(shift)
        groups.append([row_blocks(packed + jnp.where(eye, shift, 0.0)), row_blocks(ident)])
    out = []
    for shift, (left, right) in zip(shifts, eliminate(groups, lambda k: half + k, LEAF_PANEL)):
        inverse = jnp.concatenate(right, axis=0)
        upper = jnp.where(col >= row, jnp.concatenate(left, axis=0), 0.0)
        out.append((inverse, jnp.where(row < rank, upper - shift * inverse, 0.0)))
    return out


def gram_of(rows):
    return lax.dot_general(
        rows, rows, (((0,), (0,)), ((), ())), precision=HIGH, preferred_element_type=F32
    )


def times_t(a, b):
    return lax.dot_general(
        a, b, (((1,), (1,)), ((), ())), precision=HIGH, preferred_element_type=F32
    )


def keep_first(value, rank):
    row = lax.broadcasted_iota(jnp.int32, value.shape, value.ndim - 2)
    return jnp.where(row < rank, value, 0.0)


def halo_y_body(
    rank_ref, pts_ref, low_ref, high_ref, part_ref,
    sample_ref, inv_ref, proj_ref, inv1_ref, cur_ref, gram_ref,
    left_ref, base_ref, slope_ref,
):
    sides = (low_ref, high_ref)
    halo_prep(pts_ref, sides, left_ref, base_ref, slope_ref)
    for j, side in enumerate(sides):

        def step(i, carry):
            jobs = [
                (j * 8 + (i + dx) * 2 + nz, (i + dx) * 2 + nz, bz, (dx - 1, 2 * j - 1, nz - bz))
                for bz in range(2) for dx in range(3) for nz in range(2)
            ]
            halo_tiles(
                jobs, i * 4 + j * 2, part_ref, sample_ref, left_ref, side, base_ref, slope_ref
            )
            return carry

        lax.fori_loop(0, 2, step, 0)
    leaf_factor(rank_ref, sample_ref, inv_ref, proj_ref, inv1_ref, cur_ref, gram_ref)


def leaf_factor(rank_ref, sample_ref, inv_ref, proj_ref, inv1_ref, cur_ref, gram_ref):
    def group(g, carry):
        first = g * (2 * LEAF_PAIRS)
        grams = []
        for p in range(LEAF_PAIRS):
            pair = jnp.concatenate([sample_ref[first + 2 * p + k] for k in range(2)], axis=0)
            grams.append(times_t(pair, pair))
        for p, (inverse, projected) in enumerate(factor_pairs(grams, rank_ref[0])):
            for k in range(2):
                inv_ref[first + 2 * p + k] = inverse[:, k * S : k * S + S]
                proj_ref[first + 2 * p + k] = projected[:, k * S : k * S + S]
        return carry

    lax.fori_loop(0, 4 // LEAF_PAIRS, group, 0)
    gram = gram_of(proj_ref[...].reshape(8 * S, S))
    inverse, current, _ = factor_one(gram, rank_ref[1])
    inv1_ref[...] = inverse
    cur_ref[...] = current
    gram_ref[...] = gram_of(current)


def smem_spec():
    return pl.BlockSpec(memory_space=pltpu.SMEM)


def vmem_spec():
    return pl.BlockSpec(memory_space=pltpu.VMEM)


def halo_y(ranks, points, low, high, part):
    small = vmem((S, S), F32)
    many = vmem((8, S, S), F32)
    return pl.pallas_call(
        halo_y_body,
        out_shape=(vmem((8, S, N), F32), many, many, small, small, small),
        in_specs=[smem_spec()] + [vmem_spec()] * 4,
        scratch_shapes=[
            vmem((16, N, FEAT), BF16),
            vmem((8, FEAT, N), F32),
            vmem((8, FEAT, N), F32),
        ],
        name="halo_y",
    )(ranks, points, near(low), near(high), near(part))


def transfer_of(inverse, current, rank):
    return keep_first(times_t(inverse, current), rank) * math.sqrt(S)


def upper_body(height, rank_ref, g0, g1, g2, g3, *refs):
    gram = (g0[...] + g1[...]) + (g2[...] + g3[...])
    rank = rank_ref[height]
    if height == 2:
        inv1_in, proj_in, inv_ref, cur_ref, gram_ref, leaf_ref = refs
        for b in range(8):
            leaf_ref[b] = transfer_of(inv1_in[...], proj_in[b], rank_ref[1])
    elif height == 3:
        inv_in, cur_in, leaf_in, sample_in, inv_ref, cur_ref, gram_ref, done_ref, basis_ref = refs
        done_ref[...] = transfer_of(inv_in[...], cur_in[...], rank_ref[2])
        for b in range(8):
            basis = jnp.dot(leaf_in[b], sample_in[b], precision=HIGH, preferred_element_type=F32)
            basis_ref[b] = (keep_first(basis, rank_ref[0]) * math.sqrt(N)).astype(BF16)
    else:
        inv_in, cur2_in, cur_in, done_in, upper_ref, top_ref = refs
        upper_ref[0] = done_in[...]
        upper_ref[1] = transfer_of(inv_in[...], cur2_in[...], rank_ref[3])
    inverse, current, trace = factor_one(gram, rank)
    if height == 4:
        upper_ref[2] = transfer_of(inverse, cur_in[...], rank)
        top_ref[...] = current / jnp.sqrt(trace / S + TINY)
        return
    inv_ref[...] = inverse
    cur_ref[...] = current
    gram_ref[...] = gram_of(current)


def upper(height, ranks, grams, extra):
    small = vmem((S, S), F32)
    out = {
        2: (small,) * 3 + (jax.ShapeDtypeStruct((8, S, S), F32),),
        3: (small,) * 4 + (jax.ShapeDtypeStruct((8, S, N), BF16),),
        4: (jax.ShapeDtypeStruct((3, S, S), F32), jax.ShapeDtypeStruct((S, S), F32)),
    }[height]

    def body(*refs):
        upper_body(height, *refs)

    return pl.pallas_call(
        body,
        out_shape=out,
        in_specs=[smem_spec()] + [vmem_spec()] * (4 + len(extra)),
        name="upper" + str(height),
    )(ranks, *(near(value) for value in (*grams, *extra)))


def shift_pair(head, tail, axis):
    count = lax.axis_size(axis)
    up = [(i, i + 1) for i in range(count - 1)]
    down = [(i + 1, i) for i in range(count - 1)]
    return lax.ppermute(tail, axis, up), lax.ppermute(head, axis, down)


def siblings(value, flip_leaf, flip_brick):
    rows, cols = lax.axis_size("leaf"), lax.axis_size("brick")
    out = [value]
    for dx, dy in ((0, flip_brick), (flip_leaf, 0), (flip_leaf, flip_brick)):
        perm = [
            (i * cols + j, (i ^ dx) * cols + (j ^ dy)) for i in range(rows) for j in range(cols)
        ]
        out.append(lax.ppermute(value, ("leaf", "brick"), perm))
    return out


def shards(points, test_matrix, trunc_ranks):
    packed = jnp.concatenate([test_matrix, points], axis=3)
    rows = S + 3
    own_points = points.reshape(8, 3, N)
    own_tests = test_matrix.reshape(8, S, N)
    low, high = shift_pair(packed[:1], packed[1:], "leaf")
    part = own_pairs(own_points, own_tests)
    low, high, part = lax.optimization_barrier((low, high, part))
    wide = [low, packed, high]
    south = jnp.concatenate([w[:, :1] for w in wide], axis=0)
    north = jnp.concatenate([w[:, 1:] for w in wide], axis=0)
    below, above = shift_pair(south, north, "brick")
    part = halo_x(own_points, low.reshape(4, rows, N), high.reshape(4, rows, N), part)
    sample, inverse, projected, inverse1, current1, gram = halo_y(
        trunc_ranks, own_points, below.reshape(8, rows, N), above.reshape(8, rows, N), part
    )
    inverse2, current2, gram, transfer = upper(
        2, trunc_ranks, siblings(gram, 1, 1), (inverse1, projected)
    )
    inverse3, current3, gram, done2, basis = upper(
        3, trunc_ranks, siblings(gram, 3, 2), (inverse2, current1, inverse, sample)
    )
    uppers, top = upper(
        4, trunc_ranks, siblings(gram, 4, 4), (inverse3, current2, current3, done2)
    )
    block = points.shape[:3]
    return (
        basis.reshape(block + (S, N)),
        transfer.reshape(block + (S, S)),
        uppers[:, None, None],
        top[None, None],
    )


def solution(mesh):
    placed = (P("leaf", "brick", None, None, None), P("leaf", "brick", None, None, None), P())
    return jax.shard_map(
        shards,
        mesh=mesh,
        in_specs=placed,
        out_specs=(
            P("leaf", "brick", None, None, None),
            P("leaf", "brick", None, None, None),
            P(None, "leaf", "brick", None, None),
            P("leaf", "brick", None, None),
        ),
        check_vma=False,
    )
```

```python
import functools
import math

import jax
import jax.numpy as jnp
from jax import lax
from jax.experimental import pallas as pl
from jax.experimental.pallas import tpu as pltpu
from jax.sharding import PartitionSpec as P

LEVELS = 4
EXP_SCALE = -1.0 / math.log(2.0)
AHEAD = 1
BEHIND = 1
SHIFT_SHARE = 0.01
TINY = 1e-06
HIGH = lax.Precision.HIGHEST
F32 = jnp.float32
BF16 = jnp.bfloat16
S = 64
N = 256
FEAT = 32
LEAF_PAIRS = 4
LEAF_PANEL = 4
ONE_PANEL = 8
PAIR_PANEL = 4


def split_square(x):
    sq = x * x
    hi = sq.astype(BF16).astype(F32)
    return hi, sq - hi


def left_rows(pts):
    x = pts.astype(F32)
    hi, lo = split_square(x)
    threes = jnp.full((10, N), 3.0, F32)
    zeros = jnp.zeros((FEAT - 25, N), F32)
    return jnp.concatenate([-2.0 * x, -2.0 * x, hi, lo, x, threes, zeros], axis=0)


def right_rows(pts):
    x = pts.astype(F32)
    hi, lo = split_square(x)
    tripled = 3.0 * x
    coarse = tripled.astype(BF16).astype(F32)
    zero3 = jnp.zeros((3, N), F32)
    three3 = jnp.full((3, N), 3.0, F32)
    tail = jnp.zeros((FEAT - 25, N), F32)
    base = jnp.concatenate(
        [coarse, tripled - coarse, three3, three3, zero3, hi, lo, zero3, zero3[:1], tail], axis=0
    )
    slope = jnp.concatenate(
        [zero3] * 4 + [2.0 * three3, zero3, zero3, -2.0 * x, zero3[:1] + 1.0, tail], axis=0
    )
    return base, slope


def put_left(pts, left_ref, slot):
    left_ref[slot] = left_rows(pts).T.astype(BF16)


def put_right(pts, base_ref, slope_ref, slot):
    base, slope = right_rows(pts)
    base_ref[slot] = base
    slope_ref[slot] = slope


def offset_rows(off):
    row = lax.broadcasted_iota(jnp.int32, (FEAT, N), 0)
    ox, oy, oz = (jnp.asarray(o, F32) for o in off)
    total = ox * ox + oy * oy + oz * oz
    out = jnp.where((row == 12) | (row == 21), ox, total)
    out = jnp.where((row == 13) | (row == 22), oy, out)
    return jnp.where((row == 14) | (row == 23), oz, out)


def square_tile(left, base, slope, off):
    right = (base + offset_rows(off) * slope).astype(BF16)
    return jnp.dot(left, right, preferred_element_type=F32)


def matern(sq):
    sq = jnp.maximum(sq, 1e-30)
    scaled = sq * lax.rsqrt(sq)
    return ((1.0 + scaled) * jnp.exp2(scaled * EXP_SCALE)).astype(BF16)


def pipelined(squares, uses):
    ahead = [squares[k]() for k in range(min(AHEAD, len(squares)))]
    waiting = []
    for k in range(len(squares)):
        if k + AHEAD < len(squares):
            ahead.append(squares[k + AHEAD]())
        waiting.append((uses[k], matern(ahead.pop(0))))
        if len(waiting) > BEHIND:
            use, tile = waiting.pop(0)
            use(tile)
    for use, tile in waiting:
        use(tile)


def bits(box):
    return box >> 2, (box >> 1) & 1, box & 1


def own_pairs_body(pts_ref, tst_ref, out_ref, left_ref, base_ref, slope_ref):
    for b in range(8):
        put_left(pts_ref[b], left_ref, b)
        put_right(pts_ref[b], base_ref, slope_ref, b)
        out_ref[b] = jnp.zeros((S, N), F32)

    def square(n, b):
        nx, ny, nz = bits(n)
        bx, by, bz = bits(b)
        return square_tile(left_ref[n], base_ref[b], slope_ref[b], (nx - bx, ny - by, nz - bz))

    def use(n, b, both, tile):
        out_ref[b] = out_ref[b] + jnp.dot(tst_ref[n], tile, preferred_element_type=F32)
        if both:
            out_ref[n] = out_ref[n] + lax.dot_general(
                tst_ref[b], tile, (((1,), (1,)), ((), ())), preferred_element_type=F32
            )

    def step(i, carry):
        pairs = [
            ((first + shift) & 7, first, shift > 0) for first in (i, i + 4) for shift in range(4)
        ]
        pairs.append((i + 4, i, True))
        pipelined(
            [functools.partial(square, n, b) for n, b, _ in pairs],
            [functools.partial(use, n, b, both) for n, b, both in pairs],
        )
        return carry

    lax.fori_loop(0, 4, step, 0)


def vmem(shape, dtype):
    return pltpu.VMEM(shape, dtype)


def near(value):
    return pltpu.with_memory_space_constraint(value, pltpu.VMEM)


def own_pairs(points, tests):
    return pl.pallas_call(
        own_pairs_body,
        out_shape=vmem((8, S, N), F32),
        scratch_shapes=[
            vmem((8, N, FEAT), BF16),
            vmem((8, FEAT, N), F32),
            vmem((8, FEAT, N), F32),
        ],
        name="own_pairs",
    )(points, tests)


def halo_tiles(jobs, own, part_ref, out_ref, left_ref, halo_ref, base_ref, slope_ref):
    totals = [part_ref[own + bz] for bz in range(2)]

    def square(slot, box, bz, off):
        return square_tile(left_ref[slot], base_ref[own + bz], slope_ref[own + bz], off)

    def use(slot, box, bz, off, tile):
        tests = halo_ref[box, :S, :]
        totals[bz] = totals[bz] + jnp.dot(tests, tile, preferred_element_type=F32)

    pipelined(
        [functools.partial(square, *job) for job in jobs],
        [functools.partial(use, *job) for job in jobs],
    )
    for bz in range(2):
        out_ref[own + bz] = totals[bz]


def halo_prep(pts_ref, sides, left_ref, base_ref, slope_ref):
    count = sides[0].shape[0]
    for side, ref in enumerate(sides):
        for box in range(count):
            put_left(ref[box, S : S + 3, :], left_ref, side * count + box)
    for b in range(8):
        put_right(pts_ref[b], base_ref, slope_ref, b)


def halo_x_body(pts_ref, low_ref, high_ref, part_ref, out_ref, left_ref, base_ref, slope_ref):
    sides = (low_ref, high_ref)
    halo_prep(pts_ref, sides, left_ref, base_ref, slope_ref)
    for i, side in enumerate(sides):

        def step(j, carry):
            jobs = [
                (i * 4 + ny * 2 + nz, ny * 2 + nz, bz, (2 * i - 1, ny - j, nz - bz))
                for bz in range(2) for ny in range(2) for nz in range(2)
            ]
            halo_tiles(
                jobs, i * 4 + j * 2, part_ref, out_ref, left_ref, side, base_ref, slope_ref
            )
            return carry

        lax.fori_loop(0, 2, step, 0)


def halo_x(points, low, high, part):
    return pl.pallas_call(
        halo_x_body,
        out_shape=vmem((8, S, N), F32),
        in_specs=[vmem_spec()] * 4,
        scratch_shapes=[
            vmem((8, N, FEAT), BF16),
            vmem((8, FEAT, N), F32),
            vmem((8, FEAT, N), F32),
        ],
        name="halo_x",
    )(points, near(low), near(high), near(part))


def spread_row(block, row):
    return jnp.broadcast_to(block[row : row + 1, :], block.shape)


def minus(blocks, mults, row):
    return [b - m * row for b, m in zip(blocks, mults)]


def eliminate(groups, lane_of, panel):
    groups = [[list(blocks) for blocks in group] for group in groups]
    sub = lax.broadcasted_iota(jnp.int32, (8, 128), 0)
    for kb in range(8):
        diags = [jnp.ones((8, 128), F32) for _ in groups]
        for start in range(0, 8, panel):
            lanes = [lane_of(kb * 8 + start + j) for j in range(panel)]
            panels = [
                [
                    [jnp.take_along_axis(group[0][r], lane, axis=1) for r in range(kb, 8)]
                    for lane in lanes
                ]
                for group in groups
            ]
            for j in range(0, panel, 2):
                s = start + j
                for p, (group, cols) in enumerate(zip(groups, panels)):
                    one, two = cols[j], cols[j + 1]
                    a00 = spread_row(one[0], s)
                    a01 = spread_row(two[0], s)
                    a11 = spread_row(two[0], s + 1)
                    root0 = lax.rsqrt(a00)
                    root1 = lax.rsqrt(a00 * a11 - a01 * a01)
                    inv0 = root0 * root0
                    inv1 = (root1 * root1) * a00
                    m0 = [c * inv0 for c in one]
                    m0[0] = jnp.where(sub > s, m0[0], 0.0)
                    two = minus(two, m0, a01)
                    m1 = [c * inv1 for c in two]
                    m1[0] = jnp.where(sub > s + 1, m1[0], 0.0)
                    diags[p] = jnp.where(
                        sub == s, one[0], jnp.where(sub == s + 1, two[0], diags[p])
                    )
                    for jj in range(j + 2, panel):
                        cols[jj] = minus(cols[jj], m0, spread_row(cols[jj][0], s))
                        cols[jj] = minus(cols[jj], m1, spread_row(cols[jj][0], s + 1))
                    for blocks in group:
                        blocks[kb:] = minus(blocks[kb:], m0, spread_row(blocks[kb], s))
                        blocks[kb:] = minus(blocks[kb:], m1, spread_row(blocks[kb], s + 1))
        for p, group in enumerate(groups):
            root = lax.rsqrt(diags[p])
            for blocks in group:
                blocks[kb] = blocks[kb] * root
    return groups


def row_blocks(value):
    return [value[r * 8 : r * 8 + 8, :] for r in range(8)]


def total(value):
    return jnp.sum(jnp.sum(value, axis=0, keepdims=True), axis=1, keepdims=True)


def factor_one(gram, rank):
    row = lax.broadcasted_iota(jnp.int32, (S, S), 0)
    col = lax.broadcasted_iota(jnp.int32, (S, S), 1)
    eye = row == col
    trace = total(jnp.where(eye, gram, 0.0))
    shift = SHIFT_SHARE * trace / S + TINY
    shifted = gram + jnp.where(eye, shift, 0.0)
    both = jnp.concatenate([shifted, jnp.where(eye, 1.0, 0.0).astype(F32)], axis=1)
    done = eliminate(
        [[row_blocks(both)]], lambda k: jnp.full((8, 128), k, jnp.int32), ONE_PANEL
    )
    both = jnp.concatenate(done[0][0], axis=0)
    inverse = both[:, S:]
    upper = jnp.where(col >= row, both[:, :S], 0.0)
    projected = jnp.where(row < rank, upper - shift * inverse, 0.0)
    return inverse, projected, trace


def factor_pairs(grams, rank, panel):
    row = lax.broadcasted_iota(jnp.int32, (S, 128), 0)
    lane = lax.broadcasted_iota(jnp.int32, (S, 128), 1)
    first = lane < S
    col = lane & (S - 1)
    eye = row == col
    ident = jnp.where(eye, 1.0, 0.0).astype(F32)
    half = lax.broadcasted_iota(jnp.int32, (8, 128), 1) & S
    shifts, groups = [], []
    for packed in grams:
        diag = jnp.where(eye, packed, 0.0)
        traces = total(jnp.where(first, diag, 0.0)), total(jnp.where(first, 0.0, diag))
        shift = [SHIFT_SHARE * t / S + TINY for t in traces]
        shift = jnp.where(first, shift[0], shift[1])
        shifts.append(shift)
        groups.append([row_blocks(packed + jnp.where(eye, shift, 0.0)), row_blocks(ident)])
    out = []
    for shift, (left, right) in zip(shifts, eliminate(groups, lambda k: half + k, panel)):
        inverse = jnp.concatenate(right, axis=0)
        upper = jnp.where(col >= row, jnp.concatenate(left, axis=0), 0.0)
        out.append((inverse, jnp.where(row < rank, upper - shift * inverse, 0.0)))
    return out


def gram_of(rows):
    return lax.dot_general(
        rows, rows, (((0,), (0,)), ((), ())), precision=HIGH, preferred_element_type=F32
    )


def times_t(a, b):
    return lax.dot_general(
        a, b, (((1,), (1,)), ((), ())), precision=HIGH, preferred_element_type=F32
    )


def wide(gram):
    return jnp.concatenate([gram[: S // 2], gram[S // 2 :]], axis=1)


def square_of(value):
    return jnp.concatenate([value[:, :S], value[:, S:]], axis=0)


def send_all(gram, ref):
    value = wide(gram)
    for k in range(ref.shape[0]):
        ref[k] = value


def keep_first(value, rank):
    row = lax.broadcasted_iota(jnp.int32, value.shape, value.ndim - 2)
    return jnp.where(row < rank, value, 0.0)


def halo_y_body(
    rank_ref, pts_ref, low_ref, high_ref, part_ref,
    sample_ref, inv_ref, proj_ref, inv1_ref, cur_ref, gram_ref,
    left_ref, base_ref, slope_ref,
):
    sides = (low_ref, high_ref)
    halo_prep(pts_ref, sides, left_ref, base_ref, slope_ref)
    for j, side in enumerate(sides):

        def step(i, carry):
            jobs = [
                (j * 8 + (i + dx) * 2 + nz, (i + dx) * 2 + nz, bz, (dx - 1, 2 * j - 1, nz - bz))
                for bz in range(2) for dx in range(3) for nz in range(2)
            ]
            halo_tiles(
                jobs, i * 4 + j * 2, part_ref, sample_ref, left_ref, side, base_ref, slope_ref
            )
            return carry

        lax.fori_loop(0, 2, step, 0)
    leaf_factor(rank_ref, sample_ref, inv_ref, proj_ref, inv1_ref, cur_ref, gram_ref)


def leaf_factor(rank_ref, sample_ref, inv_ref, proj_ref, inv1_ref, cur_ref, gram_ref):
    def group(g, carry):
        first = g * (2 * LEAF_PAIRS)
        grams = []
        for p in range(LEAF_PAIRS):
            pair = jnp.concatenate([sample_ref[first + 2 * p + k] for k in range(2)], axis=0)
            both = times_t(pair, pair)
            first_box = lax.broadcasted_iota(jnp.int32, (S, 2 * S), 1) < S
            grams.append(jnp.where(first_box, both[:S], both[S:]))
        for p, (inverse, projected) in enumerate(factor_pairs(grams, rank_ref[0], LEAF_PANEL)):
            for k in range(2):
                inv_ref[first + 2 * p + k] = inverse[:, k * S : k * S + S]
                proj_ref[first + 2 * p + k] = projected[:, k * S : k * S + S]
        return carry

    lax.fori_loop(0, 4 // LEAF_PAIRS, group, 0)
    gram = gram_of(proj_ref[...].reshape(8 * S, S))
    inverse, current, _ = factor_one(gram, rank_ref[1])
    inv1_ref[...] = inverse
    cur_ref[...] = current
    send_all(gram_of(current), gram_ref)


def smem_spec():
    return pl.BlockSpec(memory_space=pltpu.SMEM)


def vmem_spec():
    return pl.BlockSpec(memory_space=pltpu.VMEM)


def halo_y(ranks, points, low, high, part):
    small = vmem((S, S), F32)
    many = vmem((8, S, S), F32)
    return pl.pallas_call(
        halo_y_body,
        out_shape=(vmem((8, S, N), F32), many, many, small, small, vmem((16, S // 2, 2 * S), F32)),
        in_specs=[smem_spec()] + [vmem_spec()] * 4,
        scratch_shapes=[
            vmem((16, N, FEAT), BF16),
            vmem((8, FEAT, N), F32),
            vmem((8, FEAT, N), F32),
        ],
        name="halo_y",
    )(ranks, points, near(low), near(high), near(part))


def transfer_of(inverse, current, rank):
    return keep_first(times_t(inverse, current), rank) * math.sqrt(S)


def transfer_of(inverse, current, rank):
    return keep_first(times_t(inverse, current), rank) * math.sqrt(S)


def upper23_body(
    rank_ref, gram_in, inv1_in, proj_in, cur1_in, leaf_in, sample_in,
    leaf_ref, basis_ref, done_ref, inv3_ref, own2_ref, cur3_ref, gram_ref, inv2_ref, cur2_ref,
):
    for b in range(8):
        leaf_ref[b] = transfer_of(inv1_in[...], proj_in[b], rank_ref[1])
        basis = jnp.dot(leaf_in[b], sample_in[b], precision=HIGH, preferred_element_type=F32)
        basis_ref[b] = (keep_first(basis, rank_ref[0]) * math.sqrt(N)).astype(BF16)
    sums = []
    for qa in range(2):
        for qb in range(2):
            corner = qa * 8 + qb * 2
            sums.append(
                (gram_in[corner] + gram_in[corner + 1]) + (gram_in[corner + 4] + gram_in[corner + 5])
            )
    grams = [
        jnp.concatenate([square_of(sums[2 * p]), square_of(sums[2 * p + 1])], axis=1)
        for p in range(2)
    ]
    for p, (inverse, current) in enumerate(factor_pairs(grams, rank_ref[2], PAIR_PANEL)):
        for k in range(2):
            inv2_ref[2 * p + k] = inverse[:, k * S : k * S + S]
            cur2_ref[2 * p + k] = current[:, k * S : k * S + S]
    gram = gram_of(cur2_ref[...].reshape(4 * S, S))
    own = ((lax.axis_index("leaf") >> 1) & 1) * 2 + ((lax.axis_index("brick") >> 1) & 1)
    done_ref[...] = transfer_of(inv2_ref[own], cur1_in[...], rank_ref[2])
    own2_ref[...] = cur2_ref[own]
    inverse, current, _ = factor_one(gram, rank_ref[3])
    inv3_ref[...] = inverse
    cur3_ref[...] = current
    send_all(gram_of(current), gram_ref)


def upper23(ranks, *values):
    small = vmem((S, S), F32)
    return pl.pallas_call(
        upper23_body,
        out_shape=(
            jax.ShapeDtypeStruct((8, S, S), F32),
            jax.ShapeDtypeStruct((8, S, N), BF16),
            small, small, small, small,
            vmem((4, S // 2, 2 * S), F32),
        ),
        in_specs=[smem_spec()] + [vmem_spec()] * len(values),
        scratch_shapes=[vmem((4, S, S), F32), vmem((4, S, S), F32)],
        name="upper23",
    )(ranks, *(near(value) for value in values))


def upper4_body(rank_ref, gram_in, inv3_in, cur2_in, cur3_in, done_in, upper_ref, top_ref):
    upper_ref[0] = done_in[...]
    upper_ref[1] = transfer_of(inv3_in[...], cur2_in[...], rank_ref[3])
    gram = square_of((gram_in[0] + gram_in[1]) + (gram_in[2] + gram_in[3]))
    inverse, current, trace = factor_one(gram, rank_ref[4])
    upper_ref[2] = transfer_of(inverse, cur3_in[...], rank_ref[4])
    top_ref[...] = current / jnp.sqrt(trace / S + TINY)


def upper4(ranks, *values):
    return pl.pallas_call(
        upper4_body,
        out_shape=(jax.ShapeDtypeStruct((3, S, S), F32), jax.ShapeDtypeStruct((S, S), F32)),
        in_specs=[smem_spec()] + [vmem_spec()] * len(values),
        name="upper4",
    )(ranks, *(near(value) for value in values))


def shift_pair(head, tail, axis):
    count = lax.axis_size(axis)
    up = [(i, i + 1) for i in range(count - 1)]
    down = [(i + 1, i) for i in range(count - 1)]
    return lax.ppermute(tail, axis, up), lax.ppermute(head, axis, down)


def spread_bits(bits):
    out = [0]
    for bit in bits:
        out = out + [value | 1 << bit for value in out]
    return out


def gather_siblings(copies, bits):
    rows, cols = lax.axis_size("leaf"), lax.axis_size("brick")
    flips = spread_bits(bits)
    groups = [
        [(i | a) * cols + (j | b) for a in flips for b in flips]
        for i in range(rows) if not i & flips[-1]
        for j in range(cols) if not j & flips[-1]
    ]
    return lax.all_to_all(copies, ("leaf", "brick"), 0, 0, axis_index_groups=groups, tiled=True)


def shards(points, test_matrix, trunc_ranks):
    packed = jnp.concatenate([test_matrix, points], axis=3)
    rows = S + 3
    own_points = points.reshape(8, 3, N)
    own_tests = test_matrix.reshape(8, S, N)
    low, high = shift_pair(packed[:1], packed[1:], "leaf")
    part = own_pairs(own_points, own_tests)
    low, high, part = lax.optimization_barrier((low, high, part))
    wide = [low, packed, high]
    south = jnp.concatenate([w[:, :1] for w in wide], axis=0)
    north = jnp.concatenate([w[:, 1:] for w in wide], axis=0)
    below, above = shift_pair(south, north, "brick")
    part = halo_x(own_points, low.reshape(4, rows, N), high.reshape(4, rows, N), part)
    sample, inverse, projected, inverse1, current1, gram = halo_y(
        trunc_ranks, own_points, below.reshape(8, rows, N), above.reshape(8, rows, N), part
    )
    transfer, basis, done2, inverse3, current2, current3, gram = upper23(
        trunc_ranks, gather_siblings(gram, (0, 1)), inverse1, projected, current1, inverse, sample
    )
    uppers, top = upper4(
        trunc_ranks, gather_siblings(gram, (2,)), inverse3, current2, current3, done2
    )
    block = points.shape[:3]
    return (
        basis.reshape(block + (S, N)),
        transfer.reshape(block + (S, S)),
        uppers[:, None, None],
        top[None, None],
    )


def solution(mesh):
    placed = (P("leaf", "brick", None, None, None), P("leaf", "brick", None, None, None), P())
    return jax.shard_map(
        shards,
        mesh=mesh,
        in_specs=placed,
        out_specs=(
            P("leaf", "brick", None, None, None),
            P("leaf", "brick", None, None, None),
            P(None, "leaf", "brick", None, None),
            P("leaf", "brick", None, None),
        ),
        check_vma=False,
    )
```

```python
import functools
import math

import jax
import jax.numpy as jnp
from jax import lax
from jax.experimental import pallas as pl
from jax.experimental.pallas import tpu as pltpu
from jax.sharding import PartitionSpec as P

LEVELS = 4
EXP_SCALE = -1.0 / math.log(2.0)
AHEAD = 1
BEHIND = 1
SHIFT_SHARE = 0.01
TINY = 1e-06
HIGH = lax.Precision.HIGHEST
F32 = jnp.float32
BF16 = jnp.bfloat16
S = 64
N = 256
FEAT = 32
LEAF_PAIRS = 4
LEAF_PANEL = 4
ONE_PANEL = 8
PAIR_PANEL = 4


def split_square(x):
    sq = x * x
    hi = sq.astype(BF16).astype(F32)
    return hi, sq - hi


def left_rows(pts):
    x = pts.astype(F32)
    hi, lo = split_square(x)
    threes = jnp.full((10, N), 3.0, F32)
    zeros = jnp.zeros((FEAT - 25, N), F32)
    return jnp.concatenate([-2.0 * x, -2.0 * x, hi, lo, x, threes, zeros], axis=0)


def right_rows(pts):
    x = pts.astype(F32)
    hi, lo = split_square(x)
    tripled = 3.0 * x
    coarse = tripled.astype(BF16).astype(F32)
    zero3 = jnp.zeros((3, N), F32)
    three3 = jnp.full((3, N), 3.0, F32)
    tail = jnp.zeros((FEAT - 25, N), F32)
    base = jnp.concatenate(
        [coarse, tripled - coarse, three3, three3, zero3, hi, lo, zero3, zero3[:1], tail], axis=0
    )
    slope = jnp.concatenate(
        [zero3] * 4 + [2.0 * three3, zero3, zero3, -2.0 * x, zero3[:1] + 1.0, tail], axis=0
    )
    return base, slope


def put_left(pts, left_ref, slot):
    left_ref[slot] = left_rows(pts).T.astype(BF16)


def put_right(pts, base_ref, slope_ref, slot):
    base, slope = right_rows(pts)
    base_ref[slot] = base
    slope_ref[slot] = slope


def offset_rows(off):
    row = lax.broadcasted_iota(jnp.int32, (FEAT, N), 0)
    ox, oy, oz = (jnp.asarray(o, F32) for o in off)
    total = ox * ox + oy * oy + oz * oz
    out = jnp.where((row == 12) | (row == 21), ox, total)
    out = jnp.where((row == 13) | (row == 22), oy, out)
    return jnp.where((row == 14) | (row == 23), oz, out)


def square_tile(left, base, slope, off):
    right = (base + offset_rows(off) * slope).astype(BF16)
    return jnp.dot(left, right, preferred_element_type=F32)


def matern(sq):
    sq = jnp.maximum(sq, 1e-30)
    scaled = sq * lax.rsqrt(sq)
    return ((1.0 + scaled) * jnp.exp2(scaled * EXP_SCALE)).astype(BF16)


def pipelined(squares, uses):
    ahead = [squares[k]() for k in range(min(AHEAD, len(squares)))]
    waiting = []
    for k in range(len(squares)):
        if k + AHEAD < len(squares):
            ahead.append(squares[k + AHEAD]())
        waiting.append((uses[k], matern(ahead.pop(0))))
        if len(waiting) > BEHIND:
            use, tile = waiting.pop(0)
            use(tile)
    for use, tile in waiting:
        use(tile)


def bits(box):
    return box >> 2, (box >> 1) & 1, box & 1


def own_pairs_body(pts_ref, tst_ref, out_ref, left_ref, base_ref, slope_ref):
    for b in range(8):
        put_left(pts_ref[b], left_ref, b)
        put_right(pts_ref[b], base_ref, slope_ref, b)
        out_ref[b] = jnp.zeros((S, N), F32)

    def square(n, b):
        nx, ny, nz = bits(n)
        bx, by, bz = bits(b)
        return square_tile(left_ref[n], base_ref[b], slope_ref[b], (nx - bx, ny - by, nz - bz))

    def use(n, b, both, tile):
        out_ref[b] = out_ref[b] + jnp.dot(tst_ref[n], tile, preferred_element_type=F32)
        if both:
            out_ref[n] = out_ref[n] + lax.dot_general(
                tst_ref[b], tile, (((1,), (1,)), ((), ())), preferred_element_type=F32
            )

    def step(i, carry):
        pairs = [
            ((first + shift) & 7, first, shift > 0) for first in (i, i + 4) for shift in range(4)
        ]
        pairs.append((i + 4, i, True))
        pipelined(
            [functools.partial(square, n, b) for n, b, _ in pairs],
            [functools.partial(use, n, b, both) for n, b, both in pairs],
        )
        return carry

    lax.fori_loop(0, 4, step, 0)


def vmem(shape, dtype):
    return pltpu.VMEM(shape, dtype)


def near(value):
    return pltpu.with_memory_space_constraint(value, pltpu.VMEM)


def own_pairs(points, tests):
    return pl.pallas_call(
        own_pairs_body,
        out_shape=vmem((8, S, N), F32),
        scratch_shapes=[
            vmem((8, N, FEAT), BF16),
            vmem((8, FEAT, N), F32),
            vmem((8, FEAT, N), F32),
        ],
        name="own_pairs",
    )(points, tests)


def pack_body(pts_ref, tst_ref, head_ref, tail_ref, south_ref, north_ref):
    for x, x_face in enumerate((head_ref, tail_ref)):
        for y, y_face in enumerate((south_ref, north_ref)):
            for z in range(2):
                box = x * 4 + y * 2 + z
                for face, slot in ((x_face, y * 2 + z), (y_face, x * 2 + z)):
                    face[slot, :S, :] = tst_ref[box]
                    face[slot, S : S + 3, :] = pts_ref[box]


def pack(points, tests):
    return pl.pallas_call(
        pack_body, out_shape=(vmem((4, S + 3, N), BF16),) * 4, name="pack"
    )(points, tests)


def edges_body(low_ref, high_ref, south_in, north_in, south_ref, north_ref):
    for y, (mid, out) in enumerate(((south_in, south_ref), (north_in, north_ref))):
        for z in range(2):
            out[z] = low_ref[y * 2 + z]
            out[6 + z] = high_ref[y * 2 + z]
        for slot in range(4):
            out[2 + slot] = mid[slot]


def edges(*values):
    return pl.pallas_call(
        edges_body,
        out_shape=(vmem((8, S + 3, N), BF16),) * 2,
        in_specs=[vmem_spec()] * len(values),
        name="edges",
    )(*(near(value) for value in values))


def halo_tiles(jobs, own, part_ref, out_ref, left_ref, halo_ref, base_ref, slope_ref):
    totals = [part_ref[own + bz] for bz in range(2)]

    def square(slot, box, bz, off):
        return square_tile(left_ref[slot], base_ref[own + bz], slope_ref[own + bz], off)

    def use(slot, box, bz, off, tile):
        tests = halo_ref[box, :S, :]
        totals[bz] = totals[bz] + jnp.dot(tests, tile, preferred_element_type=F32)

    pipelined(
        [functools.partial(square, *job) for job in jobs],
        [functools.partial(use, *job) for job in jobs],
    )
    for bz in range(2):
        out_ref[own + bz] = totals[bz]


def halo_prep(sides, left_ref):
    count = sides[0].shape[0]
    for side, ref in enumerate(sides):
        for box in range(count):
            put_left(ref[box, S : S + 3, :], left_ref, side * count + box)


def halo_x_body(pts_ref, low_ref, high_ref, part_ref, out_ref, left_ref, base_ref, slope_ref):
    sides = (low_ref, high_ref)
    halo_prep(sides, left_ref)
    for b in range(8):
        put_right(pts_ref[b], base_ref, slope_ref, b)
    for i, side in enumerate(sides):

        def step(j, carry):
            jobs = [
                (i * 4 + ny * 2 + nz, ny * 2 + nz, bz, (2 * i - 1, ny - j, nz - bz))
                for bz in range(2) for ny in range(2) for nz in range(2)
            ]
            halo_tiles(
                jobs, i * 4 + j * 2, part_ref, out_ref, left_ref, side, base_ref, slope_ref
            )
            return carry

        lax.fori_loop(0, 2, step, 0)


def halo_x(points, *values):
    return pl.pallas_call(
        halo_x_body,
        out_shape=vmem((8, S, N), F32),
        in_specs=[vmem_spec()] * (1 + len(values)),
        scratch_shapes=[
            vmem((8, N, FEAT), BF16),
            vmem((8, FEAT, N), F32),
            vmem((8, FEAT, N), F32),
        ],
        name="halo_x",
    )(points, *(near(value) for value in values))


def spread_row(block, row):
    return jnp.broadcast_to(block[row : row + 1, :], block.shape)


def minus(blocks, mults, row):
    return [b - m * row for b, m in zip(blocks, mults)]


def eliminate(groups, lane_of, panel):
    groups = [[list(blocks) for blocks in group] for group in groups]
    sub = lax.broadcasted_iota(jnp.int32, (8, 128), 0)
    for kb in range(8):
        diags = [jnp.ones((8, 128), F32) for _ in groups]
        for start in range(0, 8, panel):
            lanes = [lane_of(kb * 8 + start + j) for j in range(panel)]
            panels = [
                [
                    [jnp.take_along_axis(group[0][r], lane, axis=1) for r in range(kb, 8)]
                    for lane in lanes
                ]
                for group in groups
            ]
            for j in range(0, panel, 2):
                s = start + j
                for p, (group, cols) in enumerate(zip(groups, panels)):
                    one, two = cols[j], cols[j + 1]
                    a00 = spread_row(one[0], s)
                    a01 = spread_row(two[0], s)
                    a11 = spread_row(two[0], s + 1)
                    root0 = lax.rsqrt(a00)
                    root1 = lax.rsqrt(a00 * a11 - a01 * a01)
                    inv0 = root0 * root0
                    inv1 = (root1 * root1) * a00
                    m0 = [c * inv0 for c in one]
                    m0[0] = jnp.where(sub > s, m0[0], 0.0)
                    two = minus(two, m0, a01)
                    m1 = [c * inv1 for c in two]
                    m1[0] = jnp.where(sub > s + 1, m1[0], 0.0)
                    diags[p] = jnp.where(
                        sub == s, one[0], jnp.where(sub == s + 1, two[0], diags[p])
                    )
                    for jj in range(j + 2, panel):
                        cols[jj] = minus(cols[jj], m0, spread_row(cols[jj][0], s))
                        cols[jj] = minus(cols[jj], m1, spread_row(cols[jj][0], s + 1))
                    for blocks in group:
                        blocks[kb:] = minus(blocks[kb:], m0, spread_row(blocks[kb], s))
                        blocks[kb:] = minus(blocks[kb:], m1, spread_row(blocks[kb], s + 1))
        for p, group in enumerate(groups):
            root = lax.rsqrt(diags[p])
            for blocks in group:
                blocks[kb] = blocks[kb] * root
    return groups


def row_blocks(value):
    return [value[r * 8 : r * 8 + 8, :] for r in range(8)]


def total(value):
    return jnp.sum(jnp.sum(value, axis=0, keepdims=True), axis=1, keepdims=True)


def factor_one(gram, rank):
    row = lax.broadcasted_iota(jnp.int32, (S, S), 0)
    col = lax.broadcasted_iota(jnp.int32, (S, S), 1)
    eye = row == col
    trace = total(jnp.where(eye, gram, 0.0))
    shift = SHIFT_SHARE * trace / S + TINY
    shifted = gram + jnp.where(eye, shift, 0.0)
    both = jnp.concatenate([shifted, jnp.where(eye, 1.0, 0.0).astype(F32)], axis=1)
    done = eliminate(
        [[row_blocks(both)]], lambda k: jnp.full((8, 128), k, jnp.int32), ONE_PANEL
    )
    both = jnp.concatenate(done[0][0], axis=0)
    inverse = both[:, S:]
    upper = jnp.where(col >= row, both[:, :S], 0.0)
    projected = jnp.where(row < rank, upper - shift * inverse, 0.0)
    return inverse, projected, trace


def factor_pairs(grams, rank, panel):
    row = lax.broadcasted_iota(jnp.int32, (S, 128), 0)
    lane = lax.broadcasted_iota(jnp.int32, (S, 128), 1)
    first = lane < S
    col = lane & (S - 1)
    eye = row == col
    ident = jnp.where(eye, 1.0, 0.0).astype(F32)
    half = lax.broadcasted_iota(jnp.int32, (8, 128), 1) & S
    shifts, groups = [], []
    for packed in grams:
        diag = jnp.where(eye, packed, 0.0)
        traces = total(jnp.where(first, diag, 0.0)), total(jnp.where(first, 0.0, diag))
        shift = [SHIFT_SHARE * t / S + TINY for t in traces]
        shift = jnp.where(first, shift[0], shift[1])
        shifts.append(shift)
        groups.append([row_blocks(packed + jnp.where(eye, shift, 0.0)), row_blocks(ident)])
    out = []
    for shift, (left, right) in zip(shifts, eliminate(groups, lambda k: half + k, panel)):
        inverse = jnp.concatenate(right, axis=0)
        upper = jnp.where(col >= row, jnp.concatenate(left, axis=0), 0.0)
        out.append((inverse, jnp.where(row < rank, upper - shift * inverse, 0.0)))
    return out


def gram_of(rows):
    return lax.dot_general(
        rows, rows, (((0,), (0,)), ((), ())), precision=HIGH, preferred_element_type=F32
    )


def times_t(a, b):
    return lax.dot_general(
        a, b, (((1,), (1,)), ((), ())), precision=HIGH, preferred_element_type=F32
    )


def wide(gram):
    return jnp.concatenate([gram[: S // 2], gram[S // 2 :]], axis=1)


def square_of(value):
    return jnp.concatenate([value[:, :S], value[:, S:]], axis=0)


def send_all(gram, ref):
    value = wide(gram)
    for k in range(ref.shape[0]):
        ref[k] = value


def keep_first(value, rank):
    row = lax.broadcasted_iota(jnp.int32, value.shape, value.ndim - 2)
    return jnp.where(row < rank, value, 0.0)


def halo_y_body(
    rank_ref, pts_ref, low_ref, high_ref, part_ref,
    sample_ref, inv_ref, proj_ref, inv1_ref, cur_ref, gram_ref,
    left_ref, base_ref, slope_ref,
):
    sides = (low_ref, high_ref)
    halo_prep(sides, left_ref)
    for b in range(8):
        put_right(pts_ref[b], base_ref, slope_ref, b)
    for j, side in enumerate(sides):

        def step(i, carry):
            jobs = [
                (j * 8 + (i + dx) * 2 + nz, (i + dx) * 2 + nz, bz, (dx - 1, 2 * j - 1, nz - bz))
                for bz in range(2) for dx in range(3) for nz in range(2)
            ]
            halo_tiles(
                jobs, i * 4 + j * 2, part_ref, sample_ref, left_ref, side, base_ref, slope_ref
            )
            return carry

        lax.fori_loop(0, 2, step, 0)
    leaf_factor(rank_ref, sample_ref, inv_ref, proj_ref, inv1_ref, cur_ref, gram_ref)


def leaf_factor(rank_ref, sample_ref, inv_ref, proj_ref, inv1_ref, cur_ref, gram_ref):
    def group(g, carry):
        first = g * (2 * LEAF_PAIRS)
        grams = []
        for p in range(LEAF_PAIRS):
            pair = jnp.concatenate([sample_ref[first + 2 * p + k] for k in range(2)], axis=0)
            both = times_t(pair, pair)
            first_box = lax.broadcasted_iota(jnp.int32, (S, 2 * S), 1) < S
            grams.append(jnp.where(first_box, both[:S], both[S:]))
        for p, (inverse, projected) in enumerate(factor_pairs(grams, rank_ref[0], LEAF_PANEL)):
            for k in range(2):
                inv_ref[first + 2 * p + k] = inverse[:, k * S : k * S + S]
                proj_ref[first + 2 * p + k] = projected[:, k * S : k * S + S]
        return carry

    lax.fori_loop(0, 4 // LEAF_PAIRS, group, 0)
    gram = gram_of(proj_ref[...].reshape(8 * S, S))
    inverse, current, _ = factor_one(gram, rank_ref[1])
    inv1_ref[...] = inverse
    cur_ref[...] = current
    send_all(gram_of(current), gram_ref)


def smem_spec():
    return pl.BlockSpec(memory_space=pltpu.SMEM)


def vmem_spec():
    return pl.BlockSpec(memory_space=pltpu.VMEM)


def halo_y(ranks, points, *values):
    small = vmem((S, S), F32)
    many = vmem((8, S, S), F32)
    return pl.pallas_call(
        halo_y_body,
        out_shape=(vmem((8, S, N), F32), many, many, small, small, vmem((16, S // 2, 2 * S), F32)),
        in_specs=[smem_spec()] + [vmem_spec()] * (1 + len(values)),
        scratch_shapes=[
            vmem((16, N, FEAT), BF16),
            vmem((8, FEAT, N), F32),
            vmem((8, FEAT, N), F32),
        ],
        name="halo_y",
    )(ranks, points, *(near(value) for value in values))


def transfer_of(inverse, current, rank):
    return keep_first(times_t(inverse, current), rank) * math.sqrt(S)


def transfer_of(inverse, current, rank):
    return keep_first(times_t(inverse, current), rank) * math.sqrt(S)


def upper23_body(
    rank_ref, gram_in, inv1_in, proj_in, cur1_in, leaf_in, sample_in,
    leaf_ref, basis_ref, done_ref, inv3_ref, own2_ref, cur3_ref, gram_ref, inv2_ref, cur2_ref,
):
    for b in range(8):
        leaf_ref[b] = transfer_of(inv1_in[...], proj_in[b], rank_ref[1])
        basis = jnp.dot(leaf_in[b], sample_in[b], precision=HIGH, preferred_element_type=F32)
        basis_ref[b] = (keep_first(basis, rank_ref[0]) * math.sqrt(N)).astype(BF16)
    sums = []
    for qa in range(2):
        for qb in range(2):
            corner = qa * 8 + qb * 2
            sums.append(
                (gram_in[corner] + gram_in[corner + 1]) + (gram_in[corner + 4] + gram_in[corner + 5])
            )
    grams = [
        jnp.concatenate([square_of(sums[2 * p]), square_of(sums[2 * p + 1])], axis=1)
        for p in range(2)
    ]
    for p, (inverse, current) in enumerate(factor_pairs(grams, rank_ref[2], PAIR_PANEL)):
        for k in range(2):
            inv2_ref[2 * p + k] = inverse[:, k * S : k * S + S]
            cur2_ref[2 * p + k] = current[:, k * S : k * S + S]
    gram = gram_of(cur2_ref[...].reshape(4 * S, S))
    own = ((lax.axis_index("leaf") >> 1) & 1) * 2 + ((lax.axis_index("brick") >> 1) & 1)
    done_ref[...] = transfer_of(inv2_ref[own], cur1_in[...], rank_ref[2])
    own2_ref[...] = cur2_ref[own]
    inverse, current, _ = factor_one(gram, rank_ref[3])
    inv3_ref[...] = inverse
    cur3_ref[...] = current
    send_all(gram_of(current), gram_ref)


def upper23(ranks, *values):
    small = vmem((S, S), F32)
    return pl.pallas_call(
        upper23_body,
        out_shape=(
            jax.ShapeDtypeStruct((8, S, S), F32),
            jax.ShapeDtypeStruct((8, S, N), BF16),
            small, small, small, small,
            vmem((4, S // 2, 2 * S), F32),
        ),
        in_specs=[smem_spec()] + [vmem_spec()] * len(values),
        scratch_shapes=[vmem((4, S, S), F32), vmem((4, S, S), F32)],
        name="upper23",
    )(ranks, *(near(value) for value in values))


def upper4_body(rank_ref, gram_in, inv3_in, cur2_in, cur3_in, done_in, upper_ref, top_ref):
    upper_ref[0] = done_in[...]
    upper_ref[1] = transfer_of(inv3_in[...], cur2_in[...], rank_ref[3])
    gram = square_of((gram_in[0] + gram_in[1]) + (gram_in[2] + gram_in[3]))
    inverse, current, trace = factor_one(gram, rank_ref[4])
    upper_ref[2] = transfer_of(inverse, cur3_in[...], rank_ref[4])
    top_ref[...] = current / jnp.sqrt(trace / S + TINY)


def upper4(ranks, *values):
    return pl.pallas_call(
        upper4_body,
        out_shape=(jax.ShapeDtypeStruct((3, S, S), F32), jax.ShapeDtypeStruct((S, S), F32)),
        in_specs=[smem_spec()] + [vmem_spec()] * len(values),
        name="upper4",
    )(ranks, *(near(value) for value in values))


def shift_pair(head, tail, axis):
    count = lax.axis_size(axis)
    up = [(i, i + 1) for i in range(count - 1)]
    down = [(i + 1, i) for i in range(count - 1)]
    return lax.ppermute(tail, axis, up), lax.ppermute(head, axis, down)


def spread_bits(bits):
    out = [0]
    for bit in bits:
        out = out + [value | 1 << bit for value in out]
    return out


def gather_siblings(copies, bits):
    rows, cols = lax.axis_size("leaf"), lax.axis_size("brick")
    flips = spread_bits(bits)
    groups = [
        [(i | a) * cols + (j | b) for a in flips for b in flips]
        for i in range(rows) if not i & flips[-1]
        for j in range(cols) if not j & flips[-1]
    ]
    return lax.all_to_all(copies, ("leaf", "brick"), 0, 0, axis_index_groups=groups, tiled=True)


def shards(points, test_matrix, trunc_ranks):
    own_points = points.reshape(8, 3, N)
    own_tests = test_matrix.reshape(8, S, N)
    head, tail, south, north = pack(own_points, own_tests)
    low, high = shift_pair(head, tail, "leaf")
    part = own_pairs(own_points, own_tests)
    low, high, part = lax.optimization_barrier((low, high, part))
    south, north = edges(low, high, south, north)
    below, above = shift_pair(south, north, "brick")
    part = halo_x(own_points, low, high, part)
    sample, inverse, projected, inverse1, current1, gram = halo_y(
        trunc_ranks, own_points, below, above, part
    )
    transfer, basis, done2, inverse3, current2, current3, gram = upper23(
        trunc_ranks, gather_siblings(gram, (0, 1)), inverse1, projected, current1, inverse, sample
    )
    uppers, top = upper4(
        trunc_ranks, gather_siblings(gram, (2,)), inverse3, current2, current3, done2
    )
    block = points.shape[:3]
    return (
        basis.reshape(block + (S, N)),
        transfer.reshape(block + (S, S)),
        uppers[:, None, None],
        top[None, None],
    )


def solution(mesh):
    placed = (P("leaf", "brick", None, None, None), P("leaf", "brick", None, None, None), P())
    return jax.shard_map(
        shards,
        mesh=mesh,
        in_specs=placed,
        out_specs=(
            P("leaf", "brick", None, None, None),
            P("leaf", "brick", None, None, None),
            P(None, "leaf", "brick", None, None),
            P("leaf", "brick", None, None),
        ),
        check_vma=False,
    )
```
